32 devices in a mesh: energy: 2 (over x), chain: 16 (over z, y, core).
Axes of the slice: x: 2, y: 2, z: 4, core: 2. Of those that a mesh axis runs over, the one named last changes fastest.
Arguments:
- lower: bfloat16 [32, 2, 256, 256], P(('energy', 'chain')), parts along dimension 0, may hold values from -0.125 to 0.125
- upper: bfloat16 [32, 2, 256, 256], P(('energy', 'chain')), parts along dimension 0, may hold values from -0.125 to 0.125
- right_side: bfloat16 [32, 2, 256, 256], P(('energy', 'chain')), parts along dimension 0, may hold values from -6 to 6
Outputs:
- reduced_rhs: bfloat16 [32, 2, 256, 256], P(('energy', 'chain')), parts along dimension 0
The draws below stay inside these ranges and needn't reach their ends.
There are 2 independent parts, one for each index of `energy`. The reference program is written for one: setup_inputs(seed, part) draws one part's arguments, and reference() takes and returns one part's arrays. A program takes and returns all parts, laid end to end along the dimension named above; each array names one. Nothing has to cross between parts.
All inputs are finite; a program needn't handle non-finite values.
Results may differ from the reference program's by a relative error of at most 0.011.
Values may be sent and summed in bfloat16 or wider, within the bound.
A program may use at most 64 MiB of HBM per device.

```python
import jax
import jax.numpy as jnp

M = 256
COLS = 256
SECTIONS = 3
NS_STEPS = 2
ROWS = 16


def block_scale(stream_key, shape, shards, least, high):
    def one(axis_at, parts):
        steps = jax.random.uniform(jax.random.fold_in(jax.random.fold_in(stream_key, 6), axis_at), (parts,), jnp.float32, least / len(shards), high / len(shards))
        return jnp.repeat(jnp.exp(steps), shape[axis_at] // parts).reshape((-1,) + (1,) * (len(shape) - axis_at - 1))

    loudness = one(*shards[0])
    for cut in shards[1:]:
        loudness = loudness * one(*cut)
    return loudness


def scatter_about(key, extent, spread, most, split=(), kind=jnp.bfloat16):
    level = block_scale(key, extent, split, -0.22, 0.18) if split else 1.0
    entries = jax.random.normal(key, extent, jnp.float32) * spread * level
    return jnp.minimum(jnp.maximum(entries, -most), most).astype(kind)


def setup_inputs(seed: int = 0, part: int = 0) -> dict:
    arg_keys = jax.random.split(jax.random.key(seed), 4)
    part_keys = jax.random.split(jax.random.fold_in(arg_keys[3], part), 4)
    return {
        "lower": scatter_about(part_keys[0], (ROWS, 2, M, M), (7 * M) ** -0.5, 0.125, ((0, 16),)),
        "upper": scatter_about(part_keys[1], (ROWS, 2, M, M), (7 * M) ** -0.5, 0.125, ((0, 16),)),
        "right_side": scatter_about(part_keys[2], (ROWS, 2, M, COLS), 1.0, 6.0, ((0, 16),)),
    }


def complex_product(left_block, right_block):
    left_f = left_block.astype(jnp.float32)
    right_f = right_block.astype(jnp.float32)
    real_part = jnp.einsum("nij,njk->nik", left_f[:, 0], right_f[:, 0]) - jnp.einsum("nij,njk->nik", left_f[:, 1], right_f[:, 1])
    imag_part = jnp.einsum("nij,njk->nik", left_f[:, 0], right_f[:, 1]) + jnp.einsum("nij,njk->nik", left_f[:, 1], right_f[:, 0])
    return jnp.stack([real_part, imag_part], axis=1)


def from_below(values, reach):
    padding = jnp.zeros_like(values[:reach])
    return jnp.concatenate([padding, values[:-reach]], axis=0)


def from_above(values, reach):
    padding = jnp.zeros_like(values[:reach])
    return jnp.concatenate([values[reach:], padding], axis=0)


def approx_inverse(diagonal_new, identity_block):
    diagonal_low = diagonal_new.astype(jnp.bfloat16)
    approx = (2.0 * identity_block - diagonal_new).astype(jnp.bfloat16)
    for repeat in range(NS_STEPS):
        correction = (2.0 * identity_block - complex_product(diagonal_low, approx)).astype(jnp.bfloat16)
        approx = complex_product(approx, correction).astype(jnp.bfloat16)
    return approx


def reference(lower, upper, right_side):
    unit_matrix = jnp.eye(M, dtype=jnp.float32)
    identity_block = jnp.stack([unit_matrix, jnp.zeros_like(unit_matrix)])[None]
    lower_block = lower
    upper_block = upper
    current = right_side
    for number in range(SECTIONS):
        reach = 2 ** number
        final = number == SECTIONS - 1
        below_lower = from_below(lower_block, reach)
        below_upper = from_below(upper_block, reach)
        below_rhs = from_below(current, reach)
        above_lower = from_above(lower_block, reach)
        above_upper = from_above(upper_block, reach)
        above_rhs = from_above(current, reach)
        diagonal_new = identity_block - complex_product(lower_block, below_upper) - complex_product(upper_block, above_lower)
        inverse = approx_inverse(diagonal_new, identity_block)
        rhs_new = (current - complex_product(lower_block, below_rhs) - complex_product(upper_block, above_rhs)).astype(jnp.bfloat16)
        if not final:
            lower_raw = (-complex_product(lower_block, below_lower)).astype(jnp.bfloat16)
            upper_raw = (-complex_product(upper_block, above_upper)).astype(jnp.bfloat16)
            lower_block = complex_product(inverse, lower_raw).astype(jnp.bfloat16)
            upper_block = complex_product(inverse, upper_raw).astype(jnp.bfloat16)
        current = complex_product(inverse, rhs_new).astype(jnp.bfloat16)
    return current
```

```python
import functools

import jax
import jax.numpy as jnp
from jax import lax
from jax.experimental import pallas as pl
from jax.experimental.pallas import tpu as pltpu
from jax.sharding import PartitionSpec as P

NS_STEPS = 2
MESH = pl.DeviceIdType.MESH
RHS = 2


def product(left, right):
    order = left.shape[1]
    tall = left.reshape(2 * order, left.shape[2])
    by_real = jnp.dot(tall, right[0], preferred_element_type=jnp.float32)
    by_imag = jnp.dot(tall, right[1], preferred_element_type=jnp.float32)
    return by_real[:order] - by_imag[order:], by_imag[:order] + by_real[order:]


def rounded(parts):
    return jnp.stack([parts[0].astype(jnp.bfloat16), parts[1].astype(jnp.bfloat16)])


def kernel(
    quads, l_ref, u_ref, b_ref, out_ref,
    buf, new1, got1, new2, got2, last, mid,
    sem_home, sem_buf, sem_send0, sem_relay, sem_got1, sem_send1, sem_got2, sem_send2, sem_out,
):
    me = lax.axis_index("chain")
    q = me // 4
    a = (me // 2) % 2
    b = me % 2
    inner = a != b
    outer = a == b
    f = 1 - a
    g = a
    cf = 2 - a
    cg = 1 + a

    def at(quad, y, core):
        return {"chain": quad * 4 + y * 2 + core}

    mate = at(q, a, 1 - b)
    across = at(q, 1 - a, b)
    twin = at(q, b, a)
    up1, has_up1 = at(q + b, a, 1 - b), q + b < quads
    down1, has_down1 = at(q - 1 + b, a, 1 - b), q - 1 + b >= 0
    up2, has_up2 = at(q + 1, a, b), q + 1 < quads
    down2, has_down2 = at(q - 1, a, b), q >= 1
    far_step = 2 * b - 1
    far, has_far = at(q + far_step, a, 1 - b), (q + far_step >= 0) & (q + far_step < quads)
    inputs = (l_ref, u_ref, b_ref)

    home_slot = jnp.where(inner, 1 + a, 0)
    for u in range(3):
        pltpu.make_async_copy(inputs[u].at[0], buf.at[home_slot, u], sem_home.at[u]).start()

    barrier = pltpu.get_barrier_semaphore()

    def greet(who):
        pl.semaphore_signal(barrier, inc=1, device_id=who, device_id_type=MESH)

    greet(mate)
    greet(across)
    for exists, who in ((inner, twin), (has_far, far), (has_up2, up2), (has_down2, down2)):
        pl.when(exists)(functools.partial(greet, who))
    count = (
        2
        + inner.astype(jnp.int32)
        + has_far.astype(jnp.int32)
        + has_up2.astype(jnp.int32)
        + has_down2.astype(jnp.int32)
    )
    pl.semaphore_wait(barrier, count)

    def remote(src, dst, send, recv, who):
        return pltpu.make_async_remote_copy(
            src_ref=src, dst_ref=dst, send_sem=send, recv_sem=recv,
            device_id=who, device_id_type=MESH,
        )

    def send0(u, which, slot, who, half, order_u):
        return remote(
            inputs[u].at[0, half],
            buf.at[slot, u, half],
            sem_send0.at[which, u, half],
            sem_buf.at[slot, u, half],
            who,
        )

    def over_y(u, half):
        who = {"chain": jnp.where(inner, twin["chain"], across["chain"])}
        return send0(u, 0, jnp.where(inner, 0, 1 + a), who, half, None)

    def to_mate(u, half):
        return send0(u, 1, 2 - a, mate, half, None)

    def both_orders(start):
        @pl.when(a == 1)
        def _():
            for u in (0, 1, 2):
                start(u)

        @pl.when(a == 0)
        def _():
            for u in (1, 0, 2):
                start(u)

    def start_y(u):
        for half in range(2):
            over_y(u, half).start()

    both_orders(start_y)

    @pl.when(inner)
    def _():
        for u in range(3):
            for half in range(2):
                to_mate(u, half).start()

    none_far0 = outer & jnp.logical_not(has_far)
    zeros3 = jnp.zeros(buf.shape[1:], jnp.bfloat16)
    zeros2 = jnp.zeros(got2.shape[1:], jnp.bfloat16)

    @pl.when(none_far0)
    def _():
        buf[1 + a] = zeros3

    @pl.when(jnp.logical_not(has_down1))
    def _():
        got1[0] = zeros3

    @pl.when(jnp.logical_not(has_up1))
    def _():
        got1[1] = zeros3

    @pl.when(jnp.logical_not(has_down2))
    def _():
        got2[0] = zeros2

    @pl.when(jnp.logical_not(has_up2))
    def _():
        got2[1] = zeros2

    def arrive(ref, sem):
        pltpu.make_async_copy(ref, ref, sem).wait()

    def wait_home(u):
        pltpu.make_async_copy(inputs[u].at[0], buf.at[home_slot, u], sem_home.at[u]).wait()

    for u in range(3):
        wait_home(u)

    def relay(u, half):
        return remote(
            buf.at[2 - a, u, half],
            buf.at[1 + a, u, half],
            sem_relay.at[u, half],
            sem_buf.at[1 + a, u, half],
            far,
        )

    def wait_unit(u):
        for half in range(2):
            @pl.when(inner)
            def _():
                arrive(buf.at[2 - a, u, half], sem_buf.at[2 - a, u, half])

                @pl.when(has_far)
                def _():
                    relay(u, half).start()

        @pl.when(inner)
        def _():
            for half in range(2):
                arrive(buf.at[0, u, half], sem_buf.at[0, u, half])

        @pl.when(outer)
        def _():
            for half in range(2):
                arrive(buf.at[2 - a, u, half], sem_buf.at[2 - a, u, half])

    def wait_far(u):
        @pl.when(outer & has_far)
        def _():
            for half in range(2):
                arrive(buf.at[1 + a, u, half], sem_buf.at[1 + a, u, half])

    order = out_ref.shape[-1]
    row = lax.broadcasted_iota(jnp.int32, (l_ref.shape[2], l_ref.shape[3]), 0)
    col = lax.broadcasted_iota(jnp.int32, (l_ref.shape[2], l_ref.shape[3]), 1)
    unit = (row == col).astype(jnp.float32)
    del order

    def inverse(diag):
        low = rounded(diag)
        approx = rounded((2.0 * unit - diag[0], -diag[1]))
        for _ in range(NS_STEPS):
            prod = product(low, approx)
            fix = rounded((2.0 * unit - prod[0], -prod[1]))
            approx = rounded(product(approx, fix))
        return approx

    def negated(parts):
        return -parts[0], -parts[1]

    def diagonal(one, two):
        return unit - one[0] - two[0], -one[1] - two[1]

    def rhs(own, one, two):
        return rounded(
            (
                own[0].astype(jnp.float32) - one[0] - two[0],
                own[1].astype(jnp.float32) - one[1] - two[1],
            )
        )

    def send1(u, to_up):
        side = 0 if to_up else 1
        return remote(
            new1.at[u], got1.at[side, u], sem_send1.at[side, u], sem_got1.at[side, u],
            up1 if to_up else down1,
        )

    def start1(u):
        pl.when(has_up1)(lambda: send1(u, True).start())
        pl.when(has_down1)(lambda: send1(u, False).start())

    wait_unit(f)
    mid[0] = rounded(negated(product(buf[0, f], buf[cf, f])))
    wait_unit(g)
    wait_far(f)
    x = inverse(
        diagonal(product(buf[0, f], buf[cf, g]), product(buf[0, g], buf[cg, f]))
    )
    mid[2] = x
    new1[f] = rounded(product(x, mid[0]))
    start1(f)
    wait_far(g)
    mid[1] = rounded(negated(product(buf[0, g], buf[cg, g])))
    new1[g] = rounded(product(mid[2], mid[1]))
    start1(g)
    wait_unit(RHS)
    one = product(buf[0, f], buf[cf, RHS])
    wait_far(RHS)
    two = product(buf[0, g], buf[cg, RHS])
    new1[RHS] = rounded(product(mid[2], rhs(buf[0, RHS], one, two)))
    start1(RHS)

    def wait1(u):
        @pl.when(has_down1)
        def _():
            arrive(got1.at[0, u], sem_got1.at[0, u])

        @pl.when(has_up1)
        def _():
            arrive(got1.at[1, u], sem_got1.at[1, u])

    def send2(u, to_up):
        side = 0 if to_up else 1
        place = 1 if u is RHS else 0
        return remote(
            new2.at[u], got2.at[side, place], sem_send2.at[side, place],
            sem_got2.at[side, place], up2 if to_up else down2,
        )

    ef, eg = cf - 1, cg - 1
    wait1(f)
    mid[0] = rounded(negated(product(new1[f], got1[ef, f])))
    wait1(g)
    x = inverse(
        diagonal(product(new1[f], got1[ef, g]), product(new1[g], got1[eg, f]))
    )
    mid[2] = x
    new2[f] = rounded(product(x, mid[0]))

    def start2(is_upper):
        @pl.when(has_up2 & is_upper)
        def _():
            send2(1, True).start()

        @pl.when(has_down2 & jnp.logical_not(is_upper))
        def _():
            send2(0, False).start()

    start2(f == 1)
    mid[1] = rounded(negated(product(new1[g], got1[eg, g])))
    new2[g] = rounded(product(mid[2], mid[1]))
    start2(g == 1)
    wait1(RHS)
    one = product(new1[f], got1[ef, RHS])
    two = product(new1[g], got1[eg, RHS])
    new2[RHS] = rounded(product(mid[2], rhs(new1[RHS], one, two)))
    pl.when(has_up2)(lambda: send2(RHS, True).start())
    pl.when(has_down2)(lambda: send2(RHS, False).start())

    def wait2(place):
        @pl.when(has_down2)
        def _():
            arrive(got2.at[0, place], sem_got2.at[0, place])

        @pl.when(has_up2)
        def _():
            arrive(got2.at[1, place], sem_got2.at[1, place])

    wait2(0)
    x = inverse(
        diagonal(product(new2[0], got2[0, 0]), product(new2[1], got2[1, 0]))
    )
    mid[2] = x
    wait2(1)
    one = product(new2[0], got2[0, 1])
    two = product(new2[1], got2[1, 1])
    last[...] = rounded(product(mid[2], rhs(new2[RHS], one, two)))

    def home():
        return remote(last, out_ref.at[0], sem_out.at[0], sem_out.at[1], twin)

    def keep():
        return pltpu.make_async_copy(last, out_ref.at[0], sem_out.at[1])

    pl.when(inner)(lambda: home().start())
    pl.when(outer)(lambda: keep().start())

    for u in range(3):
        for half in range(2):
            over_y(u, half).wait_send()

            @pl.when(inner)
            def _(u=u, half=half):
                to_mate(u, half).wait_send()

            @pl.when(inner & has_far)
            def _(u=u, half=half):
                relay(u, half).wait_send()

        pl.when(has_up1)(lambda u=u: send1(u, True).wait_send())
        pl.when(has_down1)(lambda u=u: send1(u, False).wait_send())
    for u in (1, RHS):
        pl.when(has_up2)(lambda u=u: send2(u, True).wait_send())
    for u in (0, RHS):
        pl.when(has_down2)(lambda u=u: send2(u, False).wait_send())

    @pl.when(inner)
    def _():
        home().wait()

    pl.when(outer)(lambda: keep().wait())


def local(quads, lower, upper, right_side):
    block = lower.shape[1:]
    any_spec = pl.BlockSpec(memory_space=pl.ANY)
    low = jnp.bfloat16
    dma = pltpu.SemaphoreType.DMA
    return pl.pallas_call(
        functools.partial(kernel, quads),
        out_shape=jax.ShapeDtypeStruct(right_side.shape, right_side.dtype),
        in_specs=[any_spec] * 3,
        out_specs=any_spec,
        scratch_shapes=[
            pltpu.VMEM((3, 3, *block), low),
            pltpu.VMEM((3, *block), low),
            pltpu.VMEM((2, 3, *block), low),
            pltpu.VMEM((3, *block), low),
            pltpu.VMEM((2, 2, *block), low),
            pltpu.VMEM(block, low),
            pltpu.VMEM((3, *block), low),
            dma((3,)),
            dma((3, 3, 2)),
            dma((2, 3, 2)),
            dma((3, 2)),
            dma((2, 3)),
            dma((2, 3)),
            dma((2, 2)),
            dma((2, 2)),
            dma((2,)),
        ],
        compiler_params=pltpu.CompilerParams(collective_id=0, has_side_effects=True),
    )(lower, upper, right_side)


def solution(mesh):
    placed = P(("energy", "chain"), None, None, None)
    return jax.shard_map(
        functools.partial(local, mesh.shape["chain"] // 4),
        mesh=mesh,
        in_specs=(placed,) * 3,
        out_specs=placed,
        check_vma=False,
    )
```

```python
import functools

import jax
import jax.numpy as jnp
from jax import lax
from jax.experimental import pallas as pl
from jax.experimental.pallas import tpu as pltpu
from jax.sharding import PartitionSpec as P

NS_STEPS = 2
MESH = pl.DeviceIdType.MESH
RHS = 2


def is_rhs(u):
    return isinstance(u, int) and u >= RHS


def product(left, right):
    order = left.shape[1]
    tall = left.reshape(2 * order, left.shape[2])
    by_real = jnp.dot(tall, right[0], preferred_element_type=jnp.float32)
    by_imag = jnp.dot(tall, right[1], preferred_element_type=jnp.float32)
    return by_real[:order] - by_imag[order:], by_imag[:order] + by_real[order:]


def rounded(parts):
    return jnp.stack([parts[0].astype(jnp.bfloat16), parts[1].astype(jnp.bfloat16)])


def kernel(
    quads, l_ref, u_ref, b_ref, out_ref,
    buf, bbuf, new1, nb1, got1, gb1, new2, nb2, got2, gb2, last, mid,
    sem_home, sem_bhome, sem_buf, sem_send0, sem_relay,
    sem_got1, sem_send1, sem_got2, sem_send2, sem_out,
):
    me = lax.axis_index("chain")
    q = me // 4
    a = (me // 2) % 2
    b = me % 2
    inner = a != b
    outer = a == b
    f = 1 - a
    g = a
    cf = 2 - a
    cg = 1 + a

    def at(quad, y, core):
        return {"chain": quad * 4 + y * 2 + core}

    mate = at(q, a, 1 - b)
    across = at(q, 1 - a, b)
    twin = at(q, b, a)
    up1, has_up1 = at(q + b, a, 1 - b), q + b < quads
    down1, has_down1 = at(q - 1 + b, a, 1 - b), q - 1 + b >= 0
    up2, has_up2 = at(q + 1, a, b), q + 1 < quads
    down2, has_down2 = at(q - 1, a, b), q >= 1
    far_step = 2 * b - 1
    far, has_far = at(q + far_step, a, 1 - b), (q + far_step >= 0) & (q + far_step < quads)
    inputs = (l_ref, u_ref)
    wide = b_ref.shape[3] // 2

    def place0(slot, u, half):
        return bbuf.at[slot, half] if is_rhs(u) else buf.at[slot, u, half]

    home_slot = jnp.where(inner, 1 + a, 0)
    def load(u):
        return pltpu.make_async_copy(inputs[u].at[0], buf.at[home_slot, u], sem_home.at[u])

    def load_rhs(half, part):
        return pltpu.make_async_copy(
            b_ref.at[0, part, :, pl.ds(half * wide, wide)],
            bbuf.at[home_slot, half, :, pl.ds(part * wide, wide)],
            sem_bhome.at[half, part],
        )

    for u in (0, 1):
        load(u).start()
    for half in range(2):
        for part in range(2):
            load_rhs(half, part).start()

    barrier = pltpu.get_barrier_semaphore()

    def greet(who):
        pl.semaphore_signal(barrier, inc=1, device_id=who, device_id_type=MESH)

    greet(mate)
    greet(across)
    for exists, who in ((inner, twin), (has_far, far), (has_up2, up2), (has_down2, down2)):
        pl.when(exists)(functools.partial(greet, who))
    count = (
        2
        + inner.astype(jnp.int32)
        + has_far.astype(jnp.int32)
        + has_up2.astype(jnp.int32)
        + has_down2.astype(jnp.int32)
    )
    pl.semaphore_wait(barrier, count)

    def remote(src, dst, send, recv, who):
        return pltpu.make_async_remote_copy(
            src_ref=src, dst_ref=dst, send_sem=send, recv_sem=recv,
            device_id=who, device_id_type=MESH,
        )

    def send0(u, which, slot, who, half):
        return remote(
            bbuf.at[home_slot, half] if is_rhs(u) else inputs[u].at[0, half],
            place0(slot, u, half),
            sem_send0.at[which, u, half],
            sem_buf.at[slot, u, half],
            who,
        )

    def over_y(u, half):
        who = {"chain": jnp.where(inner, twin["chain"], across["chain"])}
        return send0(u, 0, jnp.where(inner, 0, 1 + a), who, half)

    def to_mate(u, half):
        return send0(u, 1, 2 - a, mate, half)

    def start_mate(u):
        for half in range(2):
            to_mate(u, half).start()

    def start_y(u):
        for half in range(2):
            over_y(u, half).start()

    @pl.when(inner)
    def _():
        start_mate(0)
        start_mate(1)

    @pl.when(a == 1)
    def _():
        start_y(0)
        start_y(1)

    @pl.when(a == 0)
    def _():
        start_y(1)
        start_y(0)

    for half in range(2):
        for part in range(2):
            load_rhs(half, part).wait()
    start_y(RHS)
    pl.when(inner)(lambda: start_mate(RHS))

    none_far0 = outer & jnp.logical_not(has_far)

    def clear(ref):
        ref[...] = jnp.zeros(ref.shape, ref.dtype)

    @pl.when(none_far0)
    def _():
        clear(buf.at[1 + a])
        clear(bbuf.at[1 + a])

    @pl.when(jnp.logical_not(has_down1))
    def _():
        clear(got1.at[0])
        clear(gb1.at[0])

    @pl.when(jnp.logical_not(has_up1))
    def _():
        clear(got1.at[1])
        clear(gb1.at[1])

    @pl.when(jnp.logical_not(has_down2))
    def _():
        clear(got2.at[0])
        clear(gb2.at[0])

    @pl.when(jnp.logical_not(has_up2))
    def _():
        clear(got2.at[1])
        clear(gb2.at[1])

    def arrive(ref, sem):
        pltpu.make_async_copy(ref, ref, sem).wait()

    for u in (0, 1):
        load(u).wait()

    def relay(u, half):
        return remote(
            place0(2 - a, u, half),
            place0(1 + a, u, half),
            sem_relay.at[u, half],
            sem_buf.at[1 + a, u, half],
            far,
        )

    def wait_half(u, half):
        arrive(place0(2 - a, u, half), sem_buf.at[2 - a, u, half])
        pl.when(inner & has_far)(lambda: relay(u, half).start())

    def wait_own(u, half):
        pl.when(inner)(lambda: arrive(place0(0, u, half), sem_buf.at[0, u, half]))

    def wait_unit(u):
        for half in range(2):
            wait_half(u, half)
        for half in range(2):
            wait_own(u, half)

    def wait_far(u, half):
        pl.when(outer & has_far)(
            lambda: arrive(place0(1 + a, u, half), sem_buf.at[1 + a, u, half])
        )

    row = lax.broadcasted_iota(jnp.int32, (l_ref.shape[2], l_ref.shape[3]), 0)
    col = lax.broadcasted_iota(jnp.int32, (l_ref.shape[2], l_ref.shape[3]), 1)
    unit = (row == col).astype(jnp.float32)

    def inverse(off):
        e1 = rounded(off)
        e2 = product(e1, e1)
        e2_low = rounded(e2)
        e3 = product(e1, e2_low)
        e4 = rounded(product(e2_low, e2_low))
        half_way = (unit + off[0] + e2[0] + e3[0], off[1] + e2[1] + e3[1])
        rest = product(rounded(half_way), e4)
        return rounded((half_way[0] + rest[0], half_way[1] + rest[1]))

    def negated(parts):
        return -parts[0], -parts[1]

    def coupled(one, two):
        return one[0] + two[0], one[1] + two[1]

    def by_rhs(left, right):
        order = left.shape[1]
        tall = left.reshape(2 * order, left.shape[2])
        both = jnp.dot(tall, right, preferred_element_type=jnp.float32)
        top, low = both[:order], both[order:]
        return jnp.concatenate(
            [top[:, :wide] - low[:, wide:], top[:, wide:] + low[:, :wide]], axis=1
        )

    def new_rhs(inv, own, one, two):
        return by_rhs(
            inv, (own.astype(jnp.float32) - one - two).astype(jnp.bfloat16)
        ).astype(jnp.bfloat16)

    def send1(u, to_up):
        side = 0 if to_up else 1
        rhs = is_rhs(u)
        return remote(
            nb1.at[u - RHS] if rhs else new1.at[u],
            gb1.at[side, u - RHS] if rhs else got1.at[side, u],
            sem_send1.at[side, u],
            sem_got1.at[side, u],
            up1 if to_up else down1,
        )

    def start1(u):
        pl.when(has_up1)(lambda: send1(u, True).start())
        pl.when(has_down1)(lambda: send1(u, False).start())

    wait_unit(f)
    mid[0] = rounded(negated(product(buf[0, f], buf[cf, f])))
    wait_unit(g)
    for half in range(2):
        wait_far(f, half)
    mid[2] = inverse(
        coupled(product(buf[0, f], buf[cf, g]), product(buf[0, g], buf[cg, f]))
    )
    new1[f] = rounded(product(mid[2], mid[0]))
    start1(f)
    for half in range(2):
        wait_far(g, half)
    mid[1] = rounded(negated(product(buf[0, g], buf[cg, g])))
    new1[g] = rounded(product(mid[2], mid[1]))
    start1(g)
    for half in range(2):
        wait_half(RHS, half)
    for half in range(2):
        wait_own(RHS, half)
        wait_far(RHS, half)
        one = by_rhs(buf[0, f], bbuf[cf, half])
        two = by_rhs(buf[0, g], bbuf[cg, half])
        nb1[half] = new_rhs(mid[2], bbuf[0, half], one, two)
        start1(RHS + half)

    def wait1(u):
        rhs = is_rhs(u)

        def one_side(side):
            arrive(gb1.at[side, u - RHS] if rhs else got1.at[side, u], sem_got1.at[side, u])

        pl.when(has_down1)(lambda: one_side(0))
        pl.when(has_up1)(lambda: one_side(1))

    def send2(place, to_up):
        side = 0 if to_up else 1
        return remote(
            new2.at[1 - side] if place == 0 else nb2.at[place - 1],
            got2.at[side] if place == 0 else gb2.at[side, place - 1],
            sem_send2.at[side, place],
            sem_got2.at[side, place],
            up2 if to_up else down2,
        )

    ef, eg = cf - 1, cg - 1
    wait1(f)
    mid[0] = rounded(negated(product(new1[f], got1[ef, f])))
    wait1(g)
    mid[2] = inverse(
        coupled(product(new1[f], got1[ef, g]), product(new1[g], got1[eg, f]))
    )
    new2[f] = rounded(product(mid[2], mid[0]))

    def start2(is_upper):
        pl.when(has_up2 & is_upper)(lambda: send2(0, True).start())
        pl.when(has_down2 & jnp.logical_not(is_upper))(lambda: send2(0, False).start())

    start2(f == 1)
    mid[1] = rounded(negated(product(new1[g], got1[eg, g])))
    new2[g] = rounded(product(mid[2], mid[1]))
    start2(g == 1)
    for half in range(2):
        wait1(RHS + half)
        one = by_rhs(new1[f], gb1[ef, half])
        two = by_rhs(new1[g], gb1[eg, half])
        nb2[half] = new_rhs(mid[2], nb1[half], one, two)
        pl.when(has_up2)(lambda half=half: send2(1 + half, True).start())
        pl.when(has_down2)(lambda half=half: send2(1 + half, False).start())

    def wait2(place):
        def one_side(side):
            arrive(got2.at[side] if place == 0 else gb2.at[side, place - 1], sem_got2.at[side, place])

        pl.when(has_down2)(lambda: one_side(0))
        pl.when(has_up2)(lambda: one_side(1))

    def spot(half, part):
        return (
            last.at[half, :, pl.ds(part * wide, wide)],
            out_ref.at[0, part, :, pl.ds(half * wide, wide)],
        )

    def home(half, part):
        src, dst = spot(half, part)
        return remote(src, dst, sem_out.at[0, half, part], sem_out.at[1, half, part], twin)

    def keep(half, part):
        src, dst = spot(half, part)
        return pltpu.make_async_copy(src, dst, sem_out.at[1, half, part])

    wait2(0)
    mid[2] = inverse(coupled(product(new2[0], got2[0]), product(new2[1], got2[1])))
    for half in range(2):
        wait2(1 + half)
        one = by_rhs(new2[0], gb2[0, half])
        two = by_rhs(new2[1], gb2[1, half])
        last[half] = new_rhs(mid[2], nb2[half], one, two)
        for part in range(2):
            pl.when(inner)(lambda half=half, part=part: home(half, part).start())
            pl.when(outer)(lambda half=half, part=part: keep(half, part).start())

    for u in range(3):
        for half in range(2):
            over_y(u, half).wait_send()
            pl.when(inner)(lambda u=u, half=half: to_mate(u, half).wait_send())
            pl.when(inner & has_far)(lambda u=u, half=half: relay(u, half).wait_send())
    for u in range(4):
        pl.when(has_up1)(lambda u=u: send1(u, True).wait_send())
        pl.when(has_down1)(lambda u=u: send1(u, False).wait_send())
    for place in range(3):
        pl.when(has_up2)(lambda place=place: send2(place, True).wait_send())
        pl.when(has_down2)(lambda place=place: send2(place, False).wait_send())
    for half in range(2):
        for part in range(2):
            pl.when(inner)(lambda half=half, part=part: home(half, part).wait())
            pl.when(outer)(lambda half=half, part=part: keep(half, part).wait())


def local(quads, lower, upper, right_side):
    block = lower.shape[1:]
    half = (right_side.shape[2], right_side.shape[3])
    any_spec = pl.BlockSpec(memory_space=pl.ANY)
    low = jnp.bfloat16
    dma = pltpu.SemaphoreType.DMA
    return pl.pallas_call(
        functools.partial(kernel, quads),
        out_shape=jax.ShapeDtypeStruct(right_side.shape, right_side.dtype),
        in_specs=[any_spec] * 3,
        out_specs=any_spec,
        scratch_shapes=[
            pltpu.VMEM((3, 2, *block), low),
            pltpu.VMEM((3, 2, *half), low),
            pltpu.VMEM((2, *block), low),
            pltpu.VMEM((2, *half), low),
            pltpu.VMEM((2, 2, *block), low),
            pltpu.VMEM((2, 2, *half), low),
            pltpu.VMEM((2, *block), low),
            pltpu.VMEM((2, *half), low),
            pltpu.VMEM((2, *block), low),
            pltpu.VMEM((2, 2, *half), low),
            pltpu.VMEM((2, *half), low),
            pltpu.VMEM((3, *block), low),
            dma((2,)),
            dma((2, 2)),
            dma((3, 3, 2)),
            dma((2, 3, 2)),
            dma((3, 2)),
            dma((2, 4)),
            dma((2, 4)),
            dma((2, 3)),
            dma((2, 3)),
            dma((2, 2, 2)),
        ],
        compiler_params=pltpu.CompilerParams(collective_id=0, has_side_effects=True),
    )(lower, upper, right_side)


def solution(mesh):
    placed = P(("energy", "chain"), None, None, None)
    return jax.shard_map(
        functools.partial(local, mesh.shape["chain"] // 4),
        mesh=mesh,
        in_specs=(placed,) * 3,
        out_specs=placed,
        check_vma=False,
    )
```

```python
import functools

import jax
import jax.numpy as jnp
from jax import lax
from jax.experimental import pallas as pl
from jax.experimental.pallas import tpu as pltpu
from jax.sharding import PartitionSpec as P

NS_STEPS = 2
MESH = pl.DeviceIdType.MESH
RHS = 2


def is_rhs(u):
    return isinstance(u, int) and u >= RHS


def product(left, right):
    order = left.shape[1]
    tall = left.reshape(2 * order, left.shape[2])
    by_real = jnp.dot(tall, right[0], preferred_element_type=jnp.float32)
    by_imag = jnp.dot(tall, right[1], preferred_element_type=jnp.float32)
    return by_real[:order] - by_imag[order:], by_imag[:order] + by_real[order:]


def rounded(parts):
    return jnp.stack([parts[0].astype(jnp.bfloat16), parts[1].astype(jnp.bfloat16)])


def kernel(
    quads, l_ref, u_ref, b_ref, out_ref,
    buf, bbuf, new1, nb1, got1, gb1, new2, nb2, got2, gb2, last, mid, fwd,
    sem_home, sem_bhome, sem_buf, sem_send0, sem_relay,
    sem_got1, sem_send1, sem_got2, sem_send2, sem_out, sem_fwd,
):
    me = lax.axis_index("chain")
    q = me // 4
    a = (me // 2) % 2
    b = me % 2
    inner = a != b
    outer = a == b
    f = 1 - a
    g = a
    cf = 2 - a
    cg = 1 + a

    def at(quad, y, core):
        return {"chain": quad * 4 + y * 2 + core}

    mate = at(q, a, 1 - b)
    across = at(q, 1 - a, b)
    twin = at(q, b, a)
    up1, has_up1 = at(q + b, a, 1 - b), q + b < quads
    down1, has_down1 = at(q - 1 + b, a, 1 - b), q - 1 + b >= 0
    up2, has_up2 = at(q + 1, a, b), q + 1 < quads
    down2, has_down2 = at(q - 1, a, b), q >= 1
    far_step = 2 * b - 1
    far, has_far = at(q + far_step, a, 1 - b), (q + far_step >= 0) & (q + far_step < quads)
    diag = at(q, 1 - a, 1 - b)
    pass_on = {"chain": jnp.where(a == 0, down2["chain"], up2["chain"])}
    has_far_in = ((a == 0) & has_up2) | ((a == 1) & has_down2)
    has_pass_on = outer & (((a == 0) & has_down2) | ((a == 1) & has_up2))
    inputs = (l_ref, u_ref)
    wide = b_ref.shape[3] // 2

    def place0(slot, u, half):
        return bbuf.at[slot, half] if is_rhs(u) else buf.at[slot, u, half]

    home_slot = jnp.where(inner, 1 + a, 0)
    def load(u):
        return pltpu.make_async_copy(inputs[u].at[0], buf.at[home_slot, u], sem_home.at[u])

    def load_rhs(half, part):
        return pltpu.make_async_copy(
            b_ref.at[0, part, :, pl.ds(half * wide, wide)],
            bbuf.at[home_slot, half, :, pl.ds(part * wide, wide)],
            sem_bhome.at[half, part],
        )

    for u in (0, 1):
        load(u).start()
    for half in range(2):
        for part in range(2):
            load_rhs(half, part).start()

    barrier = pltpu.get_barrier_semaphore()

    def greet(who):
        pl.semaphore_signal(barrier, inc=1, device_id=who, device_id_type=MESH)

    greet(mate)
    greet(across)
    for exists, who in ((inner, twin), (outer, diag), (has_far, far), (has_up2, up2), (has_down2, down2)):
        pl.when(exists)(functools.partial(greet, who))
    count = (
        3
        + has_far.astype(jnp.int32)
        + has_up2.astype(jnp.int32)
        + has_down2.astype(jnp.int32)
    )
    pl.semaphore_wait(barrier, count)

    def remote(src, dst, send, recv, who):
        return pltpu.make_async_remote_copy(
            src_ref=src, dst_ref=dst, send_sem=send, recv_sem=recv,
            device_id=who, device_id_type=MESH,
        )

    def send0(u, which, slot, who, half):
        return remote(
            bbuf.at[home_slot, half] if is_rhs(u) else inputs[u].at[0, half],
            place0(slot, u, half),
            sem_send0.at[which, u, half],
            sem_buf.at[slot, u, half],
            who,
        )

    def over_y(u, half):
        who = {"chain": jnp.where(inner, twin["chain"], across["chain"])}
        return send0(u, 0, jnp.where(inner, 0, 1 + a), who, half)

    def to_mate(u, half):
        return send0(u, 1, 2 - a, mate, half)

    def start_mate(u):
        for half in range(2):
            to_mate(u, half).start()

    def start_y(u):
        for half in range(2):
            over_y(u, half).start()

    @pl.when(inner)
    def _():
        start_mate(0)
        start_mate(1)

    @pl.when(a == 1)
    def _():
        start_y(0)
        start_y(1)

    @pl.when(a == 0)
    def _():
        start_y(1)
        start_y(0)

    for half in range(2):
        for part in range(2):
            load_rhs(half, part).wait()
    start_y(RHS)
    pl.when(inner)(lambda: start_mate(RHS))

    def hand_on(half):
        return remote(
            bbuf.at[0, half], fwd.at[half], sem_fwd.at[0, half], sem_fwd.at[1, half], pass_on
        )

    def hand_across(half):
        return remote(
            fwd.at[half], bbuf.at[2 - a, half], sem_fwd.at[2, half],
            sem_buf.at[2 - a, RHS, half], diag,
        )

    @pl.when(has_pass_on)
    def _():
        for half in range(2):
            hand_on(half).start()

    none_far0 = outer & jnp.logical_not(has_far)

    def clear(ref):
        ref[...] = jnp.zeros(ref.shape, ref.dtype)

    @pl.when(none_far0)
    def _():
        clear(buf.at[1 + a])
        clear(bbuf.at[1 + a])

    @pl.when(jnp.logical_not(has_down1))
    def _():
        clear(got1.at[0])
        clear(gb1.at[0])

    @pl.when(jnp.logical_not(has_up1))
    def _():
        clear(got1.at[1])
        clear(gb1.at[1])

    @pl.when(jnp.logical_not(has_down2))
    def _():
        clear(got2.at[0])
        clear(gb2.at[0])

    @pl.when(jnp.logical_not(has_up2))
    def _():
        clear(got2.at[1])
        clear(gb2.at[1])

    def arrive(ref, sem):
        pltpu.make_async_copy(ref, ref, sem).wait()

    for u in (0, 1):
        load(u).wait()

    def relay(u, half):
        return remote(
            place0(2 - a, u, half),
            place0(1 + a, u, half),
            sem_relay.at[u, half],
            sem_buf.at[1 + a, u, half],
            far,
        )

    def wait_half(u, half):
        arrive(place0(2 - a, u, half), sem_buf.at[2 - a, u, half])
        if not is_rhs(u):
            pl.when(inner & has_far)(lambda: relay(u, half).start())

    def wait_own(u, half):
        pl.when(inner)(lambda: arrive(place0(0, u, half), sem_buf.at[0, u, half]))

    def wait_unit(u):
        for half in range(2):
            wait_half(u, half)
        for half in range(2):
            wait_own(u, half)

    def wait_far(u, half):
        pl.when(outer & has_far)(
            lambda: arrive(place0(1 + a, u, half), sem_buf.at[1 + a, u, half])
        )

    row = lax.broadcasted_iota(jnp.int32, (l_ref.shape[2], l_ref.shape[3]), 0)
    col = lax.broadcasted_iota(jnp.int32, (l_ref.shape[2], l_ref.shape[3]), 1)
    unit = (row == col).astype(jnp.float32)

    def inverse(off):
        low = rounded((unit - off[0], -off[1]))
        approx = rounded((unit + off[0], off[1]))
        for _ in range(2):
            prod = product(low, approx)
            fix = rounded((2.0 * unit - prod[0], -prod[1]))
            approx = rounded(product(approx, fix))
        return approx

    def negated(parts):
        return -parts[0], -parts[1]

    def coupled(one, two):
        return one[0] + two[0], one[1] + two[1]

    def by_rhs(left, right):
        order = left.shape[1]
        tall = left.reshape(2 * order, left.shape[2])
        both = jnp.dot(tall, right, preferred_element_type=jnp.float32)
        top, low = both[:order], both[order:]
        return jnp.concatenate(
            [top[:, :wide] - low[:, wide:], top[:, wide:] + low[:, :wide]], axis=1
        )

    def new_rhs(inv, own, one, two):
        return by_rhs(
            inv, (own.astype(jnp.float32) - one - two).astype(jnp.bfloat16)
        ).astype(jnp.bfloat16)

    def send1(u, to_up):
        side = 0 if to_up else 1
        rhs = is_rhs(u)
        return remote(
            nb1.at[u - RHS] if rhs else new1.at[u],
            gb1.at[side, u - RHS] if rhs else got1.at[side, u],
            sem_send1.at[side, u],
            sem_got1.at[side, u],
            up1 if to_up else down1,
        )

    def start1(u):
        pl.when(has_up1)(lambda: send1(u, True).start())
        pl.when(has_down1)(lambda: send1(u, False).start())

    wait_unit(f)
    mid[0] = rounded(negated(product(buf[0, f], buf[cf, f])))

    @pl.when(outer & has_far_in)
    def _():
        for half in range(2):
            arrive(fwd.at[half], sem_fwd.at[1, half])
            hand_across(half).start()

    wait_unit(g)
    for half in range(2):
        wait_far(f, half)
    mid[2] = inverse(
        coupled(product(buf[0, f], buf[cf, g]), product(buf[0, g], buf[cg, f]))
    )
    new1[f] = rounded(product(mid[2], mid[0]))
    start1(f)
    for half in range(2):
        wait_far(g, half)
    mid[1] = rounded(negated(product(buf[0, g], buf[cg, g])))
    new1[g] = rounded(product(mid[2], mid[1]))
    start1(g)
    for half in range(2):
        wait_half(RHS, half)
    for half in range(2):
        wait_own(RHS, half)
        wait_far(RHS, half)
        one = by_rhs(buf[0, f], bbuf[cf, half])
        two = by_rhs(buf[0, g], bbuf[cg, half])
        nb1[half] = new_rhs(mid[2], bbuf[0, half], one, two)
        start1(RHS + half)

    def wait1(u):
        rhs = is_rhs(u)

        def one_side(side):
            arrive(gb1.at[side, u - RHS] if rhs else got1.at[side, u], sem_got1.at[side, u])

        pl.when(has_down1)(lambda: one_side(0))
        pl.when(has_up1)(lambda: one_side(1))

    def send2(place, to_up):
        side = 0 if to_up else 1
        return remote(
            new2.at[1 - side] if place == 0 else nb2.at[place - 1],
            got2.at[side] if place == 0 else gb2.at[side, place - 1],
            sem_send2.at[side, place],
            sem_got2.at[side, place],
            up2 if to_up else down2,
        )

    ef, eg = cf - 1, cg - 1
    wait1(f)
    mid[0] = rounded(negated(product(new1[f], got1[ef, f])))
    wait1(g)
    mid[2] = inverse(
        coupled(product(new1[f], got1[ef, g]), product(new1[g], got1[eg, f]))
    )
    new2[f] = rounded(product(mid[2], mid[0]))

    def start2(is_upper):
        pl.when(has_up2 & is_upper)(lambda: send2(0, True).start())
        pl.when(has_down2 & jnp.logical_not(is_upper))(lambda: send2(0, False).start())

    start2(f == 1)
    mid[1] = rounded(negated(product(new1[g], got1[eg, g])))
    new2[g] = rounded(product(mid[2], mid[1]))
    start2(g == 1)
    for half in range(2):
        wait1(RHS + half)
        one = by_rhs(new1[f], gb1[ef, half])
        two = by_rhs(new1[g], gb1[eg, half])
        nb2[half] = new_rhs(mid[2], nb1[half], one, two)
        pl.when(has_up2)(lambda half=half: send2(1 + half, True).start())
        pl.when(has_down2)(lambda half=half: send2(1 + half, False).start())

    def wait2(place):
        def one_side(side):
            arrive(got2.at[side] if place == 0 else gb2.at[side, place - 1], sem_got2.at[side, place])

        pl.when(has_down2)(lambda: one_side(0))
        pl.when(has_up2)(lambda: one_side(1))

    def spot(half, part):
        return (
            last.at[half, :, pl.ds(part * wide, wide)],
            out_ref.at[0, part, :, pl.ds(half * wide, wide)],
        )

    def home(half, part):
        src, dst = spot(half, part)
        return remote(src, dst, sem_out.at[0, half, part], sem_out.at[1, half, part], twin)

    def keep(half, part):
        src, dst = spot(half, part)
        return pltpu.make_async_copy(src, dst, sem_out.at[1, half, part])

    wait2(0)
    mid[2] = inverse(coupled(product(new2[0], got2[0]), product(new2[1], got2[1])))
    for half in range(2):
        wait2(1 + half)
        one = by_rhs(new2[0], gb2[0, half])
        two = by_rhs(new2[1], gb2[1, half])
        last[half] = new_rhs(mid[2], nb2[half], one, two)
        for part in range(2):
            pl.when(inner)(lambda half=half, part=part: home(half, part).start())
            pl.when(outer)(lambda half=half, part=part: keep(half, part).start())

    for u in range(3):
        for half in range(2):
            over_y(u, half).wait_send()
            pl.when(inner)(lambda u=u, half=half: to_mate(u, half).wait_send())
            if u != RHS:
                pl.when(inner & has_far)(lambda u=u, half=half: relay(u, half).wait_send())
    for half in range(2):
        pl.when(has_pass_on)(lambda half=half: hand_on(half).wait_send())
        pl.when(outer & has_far_in)(lambda half=half: hand_across(half).wait_send())
    for u in range(4):
        pl.when(has_up1)(lambda u=u: send1(u, True).wait_send())
        pl.when(has_down1)(lambda u=u: send1(u, False).wait_send())
    for place in range(3):
        pl.when(has_up2)(lambda place=place: send2(place, True).wait_send())
        pl.when(has_down2)(lambda place=place: send2(place, False).wait_send())
    for half in range(2):
        for part in range(2):
            pl.when(inner)(lambda half=half, part=part: home(half, part).wait())
            pl.when(outer)(lambda half=half, part=part: keep(half, part).wait())


def local(quads, lower, upper, right_side):
    block = lower.shape[1:]
    half = (right_side.shape[2], right_side.shape[3])
    any_spec = pl.BlockSpec(memory_space=pl.ANY)
    low = jnp.bfloat16
    dma = pltpu.SemaphoreType.DMA
    return pl.pallas_call(
        functools.partial(kernel, quads),
        out_shape=jax.ShapeDtypeStruct(right_side.shape, right_side.dtype),
        in_specs=[any_spec] * 3,
        out_specs=any_spec,
        scratch_shapes=[
            pltpu.VMEM((3, 2, *block), low),
            pltpu.VMEM((3, 2, *half), low),
            pltpu.VMEM((2, *block), low),
            pltpu.VMEM((2, *half), low),
            pltpu.VMEM((2, 2, *block), low),
            pltpu.VMEM((2, 2, *half), low),
            pltpu.VMEM((2, *block), low),
            pltpu.VMEM((2, *half), low),
            pltpu.VMEM((2, *block), low),
            pltpu.VMEM((2, 2, *half), low),
            pltpu.VMEM((2, *half), low),
            pltpu.VMEM((3, *block), low),
            pltpu.VMEM((2, *half), low),
            dma((2,)),
            dma((2, 2)),
            dma((3, 3, 2)),
            dma((2, 3, 2)),
            dma((3, 2)),
            dma((2, 4)),
            dma((2, 4)),
            dma((2, 3)),
            dma((2, 3)),
            dma((2, 2, 2)),
            dma((3, 2)),
        ],
        compiler_params=pltpu.CompilerParams(collective_id=0, has_side_effects=True),
    )(lower, upper, right_side)


def solution(mesh):
    placed = P(("energy", "chain"), None, None, None)
    return jax.shard_map(
        functools.partial(local, mesh.shape["chain"] // 4),
        mesh=mesh,
        in_specs=(placed,) * 3,
        out_specs=placed,
        check_vma=False,
    )
```

```python
import functools

import jax
import jax.numpy as jnp
from jax import lax
from jax.experimental import pallas as pl
from jax.experimental.pallas import tpu as pltpu
from jax.sharding import PartitionSpec as P

NS_STEPS = 2
MESH = pl.DeviceIdType.MESH
RHS = 2


def is_rhs(u):
    return isinstance(u, int) and u >= RHS


def product(left, right):
    order = left.shape[1]
    tall = left.reshape(2 * order, left.shape[2])
    by_real = jnp.dot(tall, right[0], preferred_element_type=jnp.float32)
    by_imag = jnp.dot(tall, right[1], preferred_element_type=jnp.float32)
    return by_real[:order] - by_imag[order:], by_imag[:order] + by_real[order:]


def rounded(parts):
    return jnp.stack([parts[0].astype(jnp.bfloat16), parts[1].astype(jnp.bfloat16)])


def kernel(
    quads, l_ref, u_ref, b_ref, out_ref,
    buf, bbuf, new1, nb1, got1, gb1, new2, nb2, got2, gb2, last, mid, fwd,
    sem_home, sem_bhome, sem_buf, sem_send0, sem_relay,
    sem_got1, sem_send1, sem_got2, sem_send2, sem_out, sem_fwd,
):
    me = lax.axis_index("chain")
    q = me // 4
    a = (me // 2) % 2
    b = me % 2
    inner = a != b
    outer = a == b
    f = 1 - a
    g = a
    cf = 2 - a
    cg = 1 + a

    def at(quad, y, core):
        return {"chain": quad * 4 + y * 2 + core}

    mate = at(q, a, 1 - b)
    across = at(q, 1 - a, b)
    twin = at(q, b, a)
    up1, has_up1 = at(q + b, a, 1 - b), q + b < quads
    down1, has_down1 = at(q - 1 + b, a, 1 - b), q - 1 + b >= 0
    up2, has_up2 = at(q + 1, a, b), q + 1 < quads
    down2, has_down2 = at(q - 1, a, b), q >= 1
    far_step = 2 * b - 1
    far, has_far = at(q + far_step, a, 1 - b), (q + far_step >= 0) & (q + far_step < quads)
    diag = at(q, 1 - a, 1 - b)
    pass_on = {"chain": jnp.where(a == 0, down2["chain"], up2["chain"])}
    has_far_in = ((a == 0) & has_up2) | ((a == 1) & has_down2)
    has_pass_on = outer & (((a == 0) & has_down2) | ((a == 1) & has_up2))
    inputs = (l_ref, u_ref)
    wide = b_ref.shape[3] // 2

    def place0(slot, u, half):
        return bbuf.at[slot, half] if is_rhs(u) else buf.at[slot, u, half]

    home_slot = jnp.where(inner, 1 + a, 0)
    def load(u):
        return pltpu.make_async_copy(inputs[u].at[0], buf.at[home_slot, u], sem_home.at[u])

    def load_rhs(half, part):
        return pltpu.make_async_copy(
            b_ref.at[0, part, :, pl.ds(half * wide, wide)],
            bbuf.at[home_slot, half, :, pl.ds(part * wide, wide)],
            sem_bhome.at[half, part],
        )

    for u in (0, 1):
        load(u).start()
    for half in range(2):
        for part in range(2):
            load_rhs(half, part).start()

    barrier = pltpu.get_barrier_semaphore()

    def greet(who):
        pl.semaphore_signal(barrier, inc=1, device_id=who, device_id_type=MESH)

    greet(mate)
    greet(across)
    for exists, who in ((inner, twin), (outer, diag), (has_far, far), (has_up2, up2), (has_down2, down2)):
        pl.when(exists)(functools.partial(greet, who))
    count = (
        3
        + has_far.astype(jnp.int32)
        + has_up2.astype(jnp.int32)
        + has_down2.astype(jnp.int32)
    )
    pl.semaphore_wait(barrier, count)

    def remote(src, dst, send, recv, who):
        return pltpu.make_async_remote_copy(
            src_ref=src, dst_ref=dst, send_sem=send, recv_sem=recv,
            device_id=who, device_id_type=MESH,
        )

    def send0(u, which, slot, who, half):
        return remote(
            bbuf.at[home_slot, half] if is_rhs(u) else inputs[u].at[0, half],
            place0(slot, u, half),
            sem_send0.at[which, u, half],
            sem_buf.at[slot, u, half],
            who,
        )

    def over_y(u, half):
        who = {"chain": jnp.where(inner, twin["chain"], across["chain"])}
        return send0(u, 0, jnp.where(inner, 0, 1 + a), who, half)

    def to_mate(u, half):
        return send0(u, 1, 2 - a, mate, half)

    def start_mate(u):
        for half in range(2):
            to_mate(u, half).start()

    def start_y(u):
        for half in range(2):
            over_y(u, half).start()

    @pl.when(inner)
    def _():
        start_mate(0)
        start_mate(1)

    @pl.when(a == 1)
    def _():
        start_y(0)
        start_y(1)

    @pl.when(a == 0)
    def _():
        start_y(1)
        start_y(0)

    for half in range(2):
        for part in range(2):
            load_rhs(half, part).wait()
    start_y(RHS)
    pl.when(inner)(lambda: start_mate(RHS))

    def hand_on(half):
        return remote(
            bbuf.at[0, half], fwd.at[half], sem_fwd.at[0, half], sem_fwd.at[1, half], pass_on
        )

    def hand_across(half):
        return remote(
            fwd.at[half], bbuf.at[2 - a, half], sem_fwd.at[2, half],
            sem_buf.at[2 - a, RHS, half], diag,
        )

    @pl.when(has_pass_on)
    def _():
        for half in range(2):
            hand_on(half).start()

    none_far0 = outer & jnp.logical_not(has_far)

    def clear(ref):
        ref[...] = jnp.zeros(ref.shape, ref.dtype)

    @pl.when(none_far0)
    def _():
        clear(buf.at[1 + a])
        clear(bbuf.at[1 + a])

    @pl.when(jnp.logical_not(has_down1))
    def _():
        clear(got1.at[0])
        clear(gb1.at[0])

    @pl.when(jnp.logical_not(has_up1))
    def _():
        clear(got1.at[1])
        clear(gb1.at[1])

    @pl.when(jnp.logical_not(has_down2))
    def _():
        clear(got2.at[0])
        clear(gb2.at[0])

    @pl.when(jnp.logical_not(has_up2))
    def _():
        clear(got2.at[1])
        clear(gb2.at[1])

    def arrive(ref, sem):
        pltpu.make_async_copy(ref, ref, sem).wait()

    for u in (0, 1):
        load(u).wait()

    def relay(u, half):
        return remote(
            place0(2 - a, u, half),
            place0(1 + a, u, half),
            sem_relay.at[u, half],
            sem_buf.at[1 + a, u, half],
            far,
        )

    def wait_half(u, half):
        arrive(place0(2 - a, u, half), sem_buf.at[2 - a, u, half])
        if not is_rhs(u):
            pl.when(inner & has_far)(lambda: relay(u, half).start())

    def wait_own(u, half):
        pl.when(inner)(lambda: arrive(place0(0, u, half), sem_buf.at[0, u, half]))

    def wait_unit(u):
        for half in range(2):
            wait_half(u, half)
        for half in range(2):
            wait_own(u, half)

    def wait_far(u, half):
        pl.when(outer & has_far)(
            lambda: arrive(place0(1 + a, u, half), sem_buf.at[1 + a, u, half])
        )

    row = lax.broadcasted_iota(jnp.int32, (l_ref.shape[2], l_ref.shape[3]), 0)
    col = lax.broadcasted_iota(jnp.int32, (l_ref.shape[2], l_ref.shape[3]), 1)
    unit = (row == col).astype(jnp.float32)

    def inverse(off):
        low = rounded((unit - off[0], -off[1]))
        approx = rounded((unit + off[0], off[1]))
        for _ in range(2):
            prod = product(low, approx)
            fix = rounded((2.0 * unit - prod[0], -prod[1]))
            approx = rounded(product(approx, fix))
        return approx

    def negated(parts):
        return -parts[0], -parts[1]

    def coupled(one, two):
        return one[0] + two[0], one[1] + two[1]

    def by_rhs(left, right):
        order = left.shape[1]
        tall = left.reshape(2 * order, left.shape[2])
        both = jnp.dot(tall, right, preferred_element_type=jnp.float32)
        top, low = both[:order], both[order:]
        return jnp.concatenate(
            [top[:, :wide] - low[:, wide:], top[:, wide:] + low[:, :wide]], axis=1
        )

    def new_rhs(inv, own, one, two):
        return by_rhs(
            inv, (own.astype(jnp.float32) - one - two).astype(jnp.bfloat16)
        ).astype(jnp.bfloat16)

    def send1(u, to_up):
        side = 0 if to_up else 1
        rhs = is_rhs(u)
        return remote(
            nb1.at[u - RHS] if rhs else new1.at[u],
            gb1.at[side, u - RHS] if rhs else got1.at[side, u],
            sem_send1.at[side, u],
            sem_got1.at[side, u],
            up1 if to_up else down1,
        )

    def start1(u):
        pl.when(has_up1)(lambda: send1(u, True).start())
        pl.when(has_down1)(lambda: send1(u, False).start())

    wait_unit(f)
    mid[0] = rounded(negated(product(buf[0, f], buf[cf, f])))

    @pl.when(outer & has_far_in)
    def _():
        for half in range(2):
            arrive(fwd.at[half], sem_fwd.at[1, half])
            hand_across(half).start()

    wait_unit(g)
    for half in range(2):
        wait_far(f, half)
    mid[2] = inverse(
        coupled(product(buf[0, f], buf[cf, g]), product(buf[0, g], buf[cg, f]))
    )
    new1[f] = rounded(product(mid[2], mid[0]))
    start1(f)
    for half in range(2):
        wait_far(g, half)
    mid[1] = rounded(negated(product(buf[0, g], buf[cg, g])))
    new1[g] = rounded(product(mid[2], mid[1]))
    start1(g)
    for half in range(2):
        wait_half(RHS, half)
        wait_own(RHS, half)
        wait_far(RHS, half)
        one = by_rhs(buf[0, f], bbuf[cf, half])
        two = by_rhs(buf[0, g], bbuf[cg, half])
        nb1[half] = new_rhs(mid[2], bbuf[0, half], one, two)
        start1(RHS + half)

    def wait1(u):
        rhs = is_rhs(u)

        def one_side(side):
            arrive(gb1.at[side, u - RHS] if rhs else got1.at[side, u], sem_got1.at[side, u])

        pl.when(has_down1)(lambda: one_side(0))
        pl.when(has_up1)(lambda: one_side(1))

    def send2(place, to_up):
        side = 0 if to_up else 1
        return remote(
            new2.at[1 - side] if place == 0 else nb2.at[place - 1],
            got2.at[side] if place == 0 else gb2.at[side, place - 1],
            sem_send2.at[side, place],
            sem_got2.at[side, place],
            up2 if to_up else down2,
        )

    ef, eg = cf - 1, cg - 1
    wait1(f)
    mid[0] = rounded(negated(product(new1[f], got1[ef, f])))
    wait1(g)
    mid[2] = inverse(
        coupled(product(new1[f], got1[ef, g]), product(new1[g], got1[eg, f]))
    )
    new2[f] = rounded(product(mid[2], mid[0]))

    def start2(is_upper):
        pl.when(has_up2 & is_upper)(lambda: send2(0, True).start())
        pl.when(has_down2 & jnp.logical_not(is_upper))(lambda: send2(0, False).start())

    start2(f == 1)
    mid[1] = rounded(negated(product(new1[g], got1[eg, g])))
    new2[g] = rounded(product(mid[2], mid[1]))
    start2(g == 1)
    for half in range(2):
        wait1(RHS + half)
        one = by_rhs(new1[f], gb1[ef, half])
        two = by_rhs(new1[g], gb1[eg, half])
        nb2[half] = new_rhs(mid[2], nb1[half], one, two)
        pl.when(has_up2)(lambda half=half: send2(1 + half, True).start())
        pl.when(has_down2)(lambda half=half: send2(1 + half, False).start())

    def wait2(place):
        def one_side(side):
            arrive(got2.at[side] if place == 0 else gb2.at[side, place - 1], sem_got2.at[side, place])

        pl.when(has_down2)(lambda: one_side(0))
        pl.when(has_up2)(lambda: one_side(1))

    def spot(half, part):
        return (
            last.at[half, :, pl.ds(part * wide, wide)],
            out_ref.at[0, part, :, pl.ds(half * wide, wide)],
        )

    def home(half, part):
        src, dst = spot(half, part)
        return remote(src, dst, sem_out.at[0, half, part], sem_out.at[1, half, part], twin)

    def keep(half, part):
        src, dst = spot(half, part)
        return pltpu.make_async_copy(src, dst, sem_out.at[1, half, part])

    wait2(0)
    mid[2] = inverse(coupled(product(new2[0], got2[0]), product(new2[1], got2[1])))
    for half in range(2):
        wait2(1 + half)
        one = by_rhs(new2[0], gb2[0, half])
        two = by_rhs(new2[1], gb2[1, half])
        last[half] = new_rhs(mid[2], nb2[half], one, two)
        for part in range(2):
            pl.when(inner)(lambda half=half, part=part: home(half, part).start())
            pl.when(outer)(lambda half=half, part=part: keep(half, part).start())

    for u in range(3):
        for half in range(2):
            over_y(u, half).wait_send()
            pl.when(inner)(lambda u=u, half=half: to_mate(u, half).wait_send())
            if u != RHS:
                pl.when(inner & has_far)(lambda u=u, half=half: relay(u, half).wait_send())
    for half in range(2):
        pl.when(has_pass_on)(lambda half=half: hand_on(half).wait_send())
        pl.when(outer & has_far_in)(lambda half=half: hand_across(half).wait_send())
    for u in range(4):
        pl.when(has_up1)(lambda u=u: send1(u, True).wait_send())
        pl.when(has_down1)(lambda u=u: send1(u, False).wait_send())
    for place in range(3):
        pl.when(has_up2)(lambda place=place: send2(place, True).wait_send())
        pl.when(has_down2)(lambda place=place: send2(place, False).wait_send())
    for half in range(2):
        for part in range(2):
            pl.when(inner)(lambda half=half, part=part: home(half, part).wait())
            pl.when(outer)(lambda half=half, part=part: keep(half, part).wait())


def local(quads, lower, upper, right_side):
    block = lower.shape[1:]
    half = (right_side.shape[2], right_side.shape[3])
    any_spec = pl.BlockSpec(memory_space=pl.ANY)
    low = jnp.bfloat16
    dma = pltpu.SemaphoreType.DMA
    return pl.pallas_call(
        functools.partial(kernel, quads),
        out_shape=jax.ShapeDtypeStruct(right_side.shape, right_side.dtype),
        in_specs=[any_spec] * 3,
        out_specs=any_spec,
        scratch_shapes=[
            pltpu.VMEM((3, 2, *block), low),
            pltpu.VMEM((3, 2, *half), low),
            pltpu.VMEM((2, *block), low),
            pltpu.VMEM((2, *half), low),
            pltpu.VMEM((2, 2, *block), low),
            pltpu.VMEM((2, 2, *half), low),
            pltpu.VMEM((2, *block), low),
            pltpu.VMEM((2, *half), low),
            pltpu.VMEM((2, *block), low),
            pltpu.VMEM((2, 2, *half), low),
            pltpu.VMEM((2, *half), low),
            pltpu.VMEM((3, *block), low),
            pltpu.VMEM((2, *half), low),
            dma((2,)),
            dma((2, 2)),
            dma((3, 3, 2)),
            dma((2, 3, 2)),
            dma((3, 2)),
            dma((2, 4)),
            dma((2, 4)),
            dma((2, 3)),
            dma((2, 3)),
            dma((2, 2, 2)),
            dma((3, 2)),
        ],
        compiler_params=pltpu.CompilerParams(collective_id=0, has_side_effects=True),
    )(lower, upper, right_side)


def solution(mesh):
    placed = P(("energy", "chain"), None, None, None)
    return jax.shard_map(
        functools.partial(local, mesh.shape["chain"] // 4),
        mesh=mesh,
        in_specs=(placed,) * 3,
        out_specs=placed,
        check_vma=False,
    )
```
